512 devices in a mesh: wa: 32 (over y, x_hi, core), gz: 16 (over x_lo, z).
Axes of the slice: x: 4 (x_hi: 2, x_lo: 2; x = x_hi * 2 + x_lo), y: 8, z: 8, core: 2. Of those that a mesh axis runs over, the one named last changes fastest.
Arguments:
- velocity_modes: float32 [2, 32, 512, 512], P(None, 'gz', 'wa'), may hold values from -0.03125 to 0.03125
- scalar: float32 [64, 1024, 1024], P('gz', 'wa'), may hold values from -3 to 3
- nest_shift: int32 [1], replicated, may hold values from 0 to 1023
Outputs:
- stress: bfloat16 [2, 32, 512, 512], P(None, 'gz', 'wa')
- scalar_next: float32 [64, 1024, 1024], P('gz', 'wa')
The draws below stay inside these ranges and needn't reach their ends.
Inputs may be any that keep to these rules, and one draw needn't show every extreme that they name: `nest_shift`: a shift of the fine grid along x in fine cells.
All inputs are finite; a program needn't handle non-finite values.
Results may differ from the reference program's by a relative error of at most 0.001.
Values sent between devices are 32-bit elements; how exact they have to be, the bound alone decides.
No kernel may reach another device: no remote copies, remote signals or barrier semaphores. Data moves between devices by JAX's collectives and lax.ppermute only.
A program may use at most 64 MiB of HBM per device.

```python
import math
import jax
import jax.numpy as jnp
from jax import lax

KX = 512
KY = 512
NPX = 768
NPY = 768
FX = 1024
FY = 1024
CZ = 32
FZ = 64


def steps_of(rng, shape, split, low, largest):
    gain = 1.0
    for position, shards_of in split:
        draws = jax.random.uniform(jax.random.fold_in(jax.random.fold_in(rng, 6), position), (shards_of,), jnp.float32, low / len(split), largest / len(split))
        gain = gain * jnp.repeat(jnp.exp(draws), shape[position] // shards_of).reshape((-1,) + (1,) * (len(shape) - 1 - position))
    return gain


def normal_values(own_key, shape, deviation, bound, pieces=(), kind=jnp.bfloat16):
    array = jax.random.normal(own_key, shape, jnp.float32) * deviation
    if len(pieces) > 0:
        array = steps_of(own_key, shape, pieces, -0.22, 0.18) * array
    return jnp.clip(array, min=-bound, max=bound).astype(kind)


def setup_inputs(seed: int = 0) -> dict:
    key_list = jax.random.split(jax.random.key(seed), 4)
    return {
        "velocity_modes": normal_values(key_list[0], (2, CZ, KX, KY), ((KX * KY) ** -0.5), 0.03125, ((1, 16), (2, 32)), jnp.float32),
        "scalar": normal_values(key_list[1], (FZ, FY, FX), 1.0, 3.0, ((0, 16), (1, 32)), jnp.float32),
        "nest_shift": jax.random.randint(key_list[2], (1,), 0, FX).astype(jnp.int32),
    }


kappa_base = 0.1
time_step = 0.2
highest = lax.Precision.HIGHEST

def signed_mode(number, length):
    return jnp.where(number < length // 2, number, number - length)

def hartley_table(modes_in, points, length):
    phase = jnp.mod(modes_in * points, length).astype(jnp.float32) * (2.0 * math.pi / length)
    return jnp.cos(phase) + jnp.sin(phase)

def cubic_weights(fraction):
    square = fraction * fraction
    cube = square * fraction
    return ((-cube + 2.0 * square - fraction) * 0.5, (3.0 * cube - 5.0 * square + 2.0) * 0.5, (-3.0 * cube + 4.0 * square + fraction) * 0.5, (cube - square) * 0.5)

def interp_matrix(lower, fraction, coarse_count):
    coarse = jnp.arange(coarse_count, dtype=jnp.int32)[:, None]
    weights = cubic_weights(fraction)
    matrix = jnp.zeros((coarse_count, lower.shape[0]), jnp.float32)
    for offset, weight in zip(range(-1, 3), weights):
        target = jnp.mod(lower + offset, coarse_count)
        matrix = matrix + jnp.where(coarse == target[None, :], weight[None, :], 0.0)
    return matrix

def rate(field, along_x, along_y):
    diffusivity = kappa_base * (1.0 + field * field)
    tendency = -0.5 * along_x * (jnp.roll(field, -1, 2) - jnp.roll(field, 1, 2))
    tendency = tendency - 0.5 * along_y * (jnp.roll(field, -1, 1) - jnp.roll(field, 1, 1))
    for direction in (0, 1, 2):
        face_flux = 0.5 * (diffusivity + jnp.roll(diffusivity, -1, direction)) * (jnp.roll(field, -1, direction) - field)
        tendency = tendency + face_flux - jnp.roll(face_flux, 1, direction)
    return tendency

def reference(velocity_modes, scalar, nest_shift):
    wave_x = signed_mode(jnp.arange(KX, dtype=jnp.int32), KX)
    wave_y = signed_mode(jnp.arange(KY, dtype=jnp.int32), KY)
    synth_x = hartley_table(wave_x[:, None], jnp.arange(NPX, dtype=jnp.int32)[None, :], NPX)
    synth_y = hartley_table(wave_y[:, None], jnp.arange(NPY, dtype=jnp.int32)[None, :], NPY)
    spaced = jnp.einsum('czkq,qy->czky', velocity_modes, synth_y, precision=highest)
    spaced = jnp.einsum('czky,kx->czyx', spaced, synth_x, precision=highest)
    along_x = spaced[0]
    along_y = spaced[1]
    products = jnp.stack([along_x * along_x - along_y * along_y, along_x * along_y])
    half_done = jnp.einsum('czyx,kx->czyk', products, synth_x / math.sqrt(NPX), precision=highest)
    stress = jnp.einsum('czyk,qy->czkq', half_done, synth_y / math.sqrt(NPY), precision=highest).astype(jnp.bfloat16)
    shift_cells = nest_shift[0]
    numer_x = 3 * (2 * jnp.arange(FX, dtype=jnp.int32) + 1 + 2 * shift_cells)
    matrix_x = interp_matrix(numer_x // 8, (numer_x % 8).astype(jnp.float32) / 8.0, NPX)
    numer_y = 3 * (2 * jnp.arange(FY, dtype=jnp.int32) + 1)
    matrix_y = interp_matrix(numer_y // 8, (numer_y % 8).astype(jnp.float32) / 8.0, NPY)
    numer_z = 2 * jnp.arange(FZ, dtype=jnp.int32) - 1
    matrix_z = interp_matrix(jnp.floor_divide(numer_z, 4), jnp.mod(numer_z, 4).astype(jnp.float32) / 4.0, CZ)
    fine_speed = jnp.einsum('czyx,xi->czyi', spaced, matrix_x, precision=highest)
    fine_speed = jnp.einsum('czyi,yj->czji', fine_speed, matrix_y, precision=highest)
    fine_speed = jnp.einsum('czji,zk->ckji', fine_speed, matrix_z, precision=highest)
    section = scalar + time_step * rate(scalar, fine_speed[0], fine_speed[1])
    scalar_next = 0.5 * (scalar + section + time_step * rate(section, fine_speed[0], fine_speed[1]))
    return (stress, scalar_next)
```

```python
import math

import jax
import jax.numpy as jnp
import ml_dtypes
import numpy as np
from jax import lax
from jax.experimental import pallas as pl
from jax.experimental.pallas import tpu as pltpu
from jax.sharding import PartitionSpec as P


F32 = jnp.float32
BF16 = jnp.bfloat16
N = 768
HALF = 256
OWN = 24
ROWS = 32
EXT = 40
RETAINED = (0, 1, 4, 5)
BASE = 512
PAYLOAD = BASE + 2 * 8 * EXT + 8


def split_host(array):
    high = array.astype(np.float32).astype(ml_dtypes.bfloat16)
    low = (array - high.astype(np.float64)).astype(np.float32).astype(ml_dtypes.bfloat16)
    return high, low


def cas_seeds():
    lane = np.arange(128, dtype=np.int64)
    rows = []
    for steps in (8 * np.arange(96, dtype=np.int64), np.arange(8, dtype=np.int64)):
        angle = ((steps[:, None] * lane) % N).astype(np.float64) * (2.0 * math.pi / N)
        rows += [np.cos(angle), np.sin(angle)]
    return np.concatenate(rows).astype(np.float32)


def weights_of(t):
    return (
        (-(t**3) + 2 * t**2 - t) / 2,
        (3 * t**3 - 5 * t**2 + 2) / 2,
        (-3 * t**3 + 4 * t**2 + t) / 2,
        (t**3 - t**2) / 2,
    )


def row_plane_matrix():
    along_y = np.zeros((EXT, ROWS))
    for e in range(1, 35):
        numer = 3 * (2 * (e - 2) + 1)
        for offset, weight in zip(range(-1, 3), weights_of((numer % 8) / 8.0)):
            along_y[e, numer // 8 + offset + 2] += weight
    along_z = np.zeros((6, 6))
    for k in range(6):
        numer = 2 * (k - 1) - 1
        for offset, weight in zip(range(-1, 3), weights_of((numer % 4) / 4.0)):
            along_z[k, numer // 4 + offset + 2] += weight
    full = np.einsum("kp,er->kepr", along_z, along_y).reshape(6 * EXT, 6, ROWS)
    below, own, above = (full[:, i : i + 2].reshape(6 * EXT, 64) for i in (0, 2, 4))
    none = np.zeros_like(own)
    return np.stack(
        [
            np.concatenate([below, above, own, none], axis=1),
            np.concatenate([below, above, none, own], axis=1),
        ]
    )


def mm(a, b):
    return lax.dot_general(a, b, (((1,), (0,)), ((), ())), preferred_element_type=F32)


def mm_nt(a, b):
    return lax.dot_general(a, b, (((1,), (1,)), ((), ())), preferred_element_type=F32)


def split(x):
    high = x.astype(BF16)
    low = (x - high.astype(F32)).astype(BF16)
    return high, low


def lanes_of(shape):
    return lax.broadcasted_iota(jnp.int32, shape, len(shape) - 1)


def make_table(seed_ref, fh_ref, fl_ref, blocks=(0, 1, 2, 3, 4, 5)):
    near_cos, near_sin = seed_ref[192:200, :], seed_ref[200:208, :]
    sublane = lax.broadcasted_iota(jnp.int32, (8, 128), 0)
    turns = []
    for phase in range(3):
        turns.append([])
        for b in range(6):
            sixth = lax.rem(b * (2 * phase + sublane), 6)
            cos, sin = jnp.ones((8, 128), F32), jnp.zeros((8, 128), F32)
            for i in range(1, 6):
                angle = 2.0 * math.pi * i / 6
                cos = jnp.where(sixth == i, round(math.cos(angle), 6), cos)
                sin = jnp.where(sixth == i, 0.0 if i == 3 else math.sin(angle), sin)
            turns[-1].append((cos, sin))

    def six(step, carry):
        for pair in range(3):
            parts = []
            for i in (2 * pair, 2 * pair + 1):
                m = 6 * step + i
                far_cos, far_sin = seed_ref[pl.ds(m, 1), :], seed_ref[pl.ds(96 + m, 1), :]
                cos = far_cos * near_cos - far_sin * near_sin
                sin = far_sin * near_cos + far_cos * near_sin
                plus, minus = cos + sin, cos - sin
                tiles = []
                for b in blocks:
                    turn_cos, turn_sin = turns[i % 3][b]
                    tiles.append(turn_cos * plus + turn_sin * minus if b else plus)
                parts.append(jnp.concatenate(tiles, axis=1))
            high, low = split(jnp.concatenate(parts, axis=0))
            row = pl.multiple_of(48 * step + 16 * pair, 16)
            fh_ref[pl.ds(row, 16), :] = high
            fl_ref[pl.ds(row, 16), :] = low
        return carry

    lax.fori_loop(0, 16, six, 0)


def synth_y_kernel(m_ref, seed_ref, out_ref, fh_ref, fl_ref):
    make_table(seed_ref, fh_ref, fl_ref)
    mh, ml = split(m_ref[...])
    both = jnp.concatenate([mh, ml], axis=0)
    stacked = mm(both[:, :HALF], fh_ref[0:HALF, :]) + mm(both[:, HALF:], fh_ref[512:, :])
    lines = stacked[:64] + stacked[64:]
    lines = lines + mm(mh[:, :HALF], fl_ref[0:HALF, :]) + mm(mh[:, HALF:], fl_ref[512:, :])
    tiles = [lines[:, 128 * t : 128 * t + 128] for t in range(6)]
    lane = lanes_of((64, 128))
    group = lanes_of((16, 128)) // 32
    for d in range(32):
        start = (OWN * d - 2) % N
        t, first = start // 128, start % 128
        window = tiles[t]
        if first + ROWS > 128:
            window = jnp.where(lane >= first, window, tiles[(t + 1) % 6])
        chunk = None
        for cz in range(4):
            piece = window[16 * cz : 16 * cz + 16]
            shift = (32 * cz - first) % 128
            if shift:
                piece = pltpu.roll(piece, shift, 1)
            chunk = piece if chunk is None else jnp.where(group == cz, piece, chunk)
        out_ref[16 * d : 16 * d + 16, :] = chunk


def pack_kernel(r_ref, g_ref, before_ref, after_ref, up_ref, down_ref):
    received = r_ref[...]
    for ref in (up_ref, down_ref):
        ref[0:BASE, :] = received
        ref[PAYLOAD - 8 : PAYLOAD, :] = jnp.zeros((8, 128), F32)
    for p in range(4):
        ref = down_ref if p < 2 else up_ref
        for t in range(8):
            row = BASE + ((p % 2) * 8 + t) * EXT
            columns = slice(128 * t, 128 * t + 128)
            ref[row : row + 2, :] = before_ref[2 * p : 2 * p + 2, columns]
            ref[row + 2 : row + 34, :] = g_ref[p, :, columns]
            ref[row + 34 : row + 36, :] = after_ref[2 * p : 2 * p + 2, columns]
            ref[row + 36 : row + 40, :] = jnp.zeros((4, 128), F32)


def spectral_kernel(r_ref, seed_ref, spaced_ref, out_ref, fh_ref, fl_ref):
    make_table(seed_ref, fh_ref, fl_ref)
    rh, rl = split(r_ref[0:BASE, :])
    both = jnp.concatenate([rh, rl], axis=1)
    o = mm(fh_ref[:, 0:HALF], both[0:HALF]) + mm(fh_ref[:, 512:], both[HALF:])
    spaced = o[:, :128] + o[:, 128:]
    spaced = spaced + mm(fl_ref[:, 0:HALF], rh[0:HALF]) + mm(fl_ref[:, 512:], rh[HALF:])
    spaced_ref[...] = spaced
    swapped = pltpu.roll(spaced, 64, 1)
    products = jnp.where(
        lanes_of((N, 128)) < 64,
        spaced * spaced - swapped * swapped,
        spaced * swapped,
    )
    ph, plo = split(products)
    both = jnp.concatenate([ph, plo], axis=1)
    for first, row in ((0, 0), (512, HALF)):
        o = mm(fh_ref[first : first + HALF, :], both)
        out_ref[row : row + HALF, :] = (
            o[:, :128] + o[:, 128:] + mm(fl_ref[first : first + HALF, :], ph)
        )


def analysis_y_kernel(r_ref, seed_ref, out_ref, fh_ref, fl_ref):
    make_table(seed_ref, fh_ref, fl_ref, RETAINED)
    lane = lanes_of((16, 128))
    columns = []
    for t in range(6):
        rows = []
        for cz in range(4):
            tile = None
            for d in range(32):
                low, high = OWN * d - 128 * t, OWN * d - 128 * t + OWN
                if high <= 0 or low >= 128:
                    continue
                shift = (low - (32 * cz + 2)) % 128
                piece = r_ref[16 * d : 16 * d + 16, :]
                if shift:
                    piece = pltpu.roll(piece, shift, 1)
                tile = piece if tile is None else jnp.where(lane >= low, piece, tile)
            rows.append(tile)
        columns.append(jnp.concatenate(rows, axis=0))
    lines = jnp.concatenate(columns, axis=1)
    ah, al = split(lines)
    both = jnp.concatenate([ah, al], axis=0)
    o = mm(both, fh_ref[...])
    o = o[:64] + o[64:] + mm(ah, fl_ref[...])
    out_ref[...] = (o * (1.0 / N)).astype(BF16)


def flux(g, gg, h, hh):
    return (h - g) * (gg + hh)


def fine_kernel(
    shift_ref,
    spaced_ref,
    up_ref,
    down_ref,
    low_ref,
    high_ref,
    seed_ref,
    bh_ref,
    bl_ref,
    out_ref,
    fh_ref,
    fl_ref,
    x_ref,
    u_ref,
    s_ref,
):
    make_table(seed_ref, fh_ref, fl_ref, RETAINED)
    below = low_ref[0:BASE, :]
    above = high_ref[0:BASE, :]
    left = lanes_of((BASE, 128)) < 64
    first = jnp.where(left, below, pltpu.roll(above, 64, 1))
    second = jnp.where(left, pltpu.roll(below, 64, 1), above)
    rh, rl = split(jnp.concatenate([first, second], axis=1))
    halo = mm(fh_ref[...], rh) + mm(fh_ref[...], rl) + mm(fl_ref[...], rh)
    for i, tile in enumerate((halo[:, :128], halo[:, 128:], spaced_ref[...])):
        x_ref[i, 0:N, :] = tile
        x_ref[i, N : N + 128, :] = tile[0:128]

    shift = shift_ref[0]
    base = lax.shift_right_arithmetic(3 * (1 + 2 * shift), 3) - 1
    cell = lax.broadcasted_iota(jnp.int32, (128, 128), 0)
    coarse = lanes_of((128, 128))
    numer = 3 * (2 * cell + 1 + 2 * shift)
    lower = lax.shift_right_arithmetic(numer, 3) - base
    t = jnp.bitwise_and(numer, 7).astype(F32) * 0.125
    square = t * t
    cube = square * t
    weights = (
        (-cube + 2.0 * square - t) * 0.5,
        (3.0 * cube - 5.0 * square + 2.0) * 0.5,
        (-3.0 * cube + 4.0 * square + t) * 0.5,
        (cube - square) * 0.5,
    )
    matrix = jnp.zeros((128, 128), F32)
    for offset, weight in zip(range(-1, 3), weights):
        matrix = matrix + jnp.where(coarse == lower + offset, weight, 0.0)
    wh, wl = split(matrix)
    both = jnp.concatenate([wh, wl], axis=0)

    for pair in range(4):
        lines = []
        for b in (2 * pair, 2 * pair + 1):
            start = lax.rem(base + N + 96 * b, N)
            window = jnp.concatenate([x_ref[i, pl.ds(start, 128), :] for i in range(3)], axis=1)
            vh, vl = split(window)
            o = mm(both, vh)
            lines.append(o[:128] + o[128:] + mm(wh, vl))
        lines = jnp.concatenate(lines, axis=0)
        for c in range(2):
            mine = jnp.concatenate([lines[:, 128 * c : 128 * c + 128], lines[:, 256:]], axis=1)
            vh, vl = split(mine)
            o = mm_nt(bh_ref[c], vh) + mm_nt(bl_ref[c], vh) + mm_nt(bh_ref[c], vl)
            u_ref[c, 2 * pair] = o[:, :128]
            u_ref[c, 2 * pair + 1] = o[:, 128:]

    homes = ((low_ref, 0), (low_ref, 1), (down_ref, 0), (down_ref, 1))
    homes = homes + ((up_ref, 0), (up_ref, 1), (high_ref, 0), (high_ref, 1))

    def around(centre, west, east):
        lane = lanes_of(centre.shape)
        to_east = jnp.where(lane == 127, pltpu.roll(east, 127, 1), pltpu.roll(centre, 127, 1))
        to_west = jnp.where(lane == 0, pltpu.roll(west, 1, 1), pltpu.roll(centre, 1, 1))
        return to_west, to_east

    def rate(load, planes, count, skip, use):
        def one(t, carry):
            west_t = lax.rem(t + 7, 8)
            east_t = lax.rem(t + 1, 8)
            first = planes[0]
            g = load(first, t, skip, count)
            gg = 1.0 + g * g
            below = load(first - 1, t, skip, count)
            lower = flux(below, 1.0 + below * below, g, gg)
            for p in planes:
                above = load(p + 1, t, skip, count)
                aa = 1.0 + above * above
                upper = flux(g, gg, above, aa)
                north = load(p, t, skip + 1, count)
                south = load(p, t, skip - 1, count)
                west, east = around(
                    g, load(p, west_t, skip, count), load(p, east_t, skip, count)
                )
                total = flux(g, gg, north, 1.0 + north * north) + flux(
                    g, gg, south, 1.0 + south * south
                )
                total = total + flux(g, gg, east, 1.0 + east * east)
                total = total + flux(g, gg, west, 1.0 + west * west)
                total = total + upper - lower
                row = (p - 1) * EXT + skip
                along_x = u_ref[0, t, row : row + count, :]
                along_y = u_ref[1, t, row : row + count, :]
                wind = along_x * (east - west) + along_y * (north - south)
                use(p, t, g, g + (0.01 * total - 0.1 * wind))
                lower, g, gg = upper, above, aa
            return carry

        lax.fori_loop(0, 8, one, 0)

    def load_scalar(p, t, skip, count):
        ref, plane = homes[p]
        row = pl.multiple_of(BASE + (plane * 8 + t) * EXT, 8)
        return ref[pl.ds(row + skip, count), :]

    def load_section(p, t, skip, count):
        row = pl.multiple_of(((p - 1) * 8 + t) * EXT, 8)
        return s_ref[pl.ds(row + skip, count), :]

    def keep_section(p, t, g, result):
        row = pl.multiple_of(((p - 1) * 8 + t) * EXT, 8)
        s_ref[pl.ds(row, EXT), :] = result

    def keep_result(p, t, g, result):
        scalar = load_scalar(p, t, 2, 32)
        column = pl.multiple_of(t * 128, 128)
        out_ref[p - 2, :, pl.ds(column, 128)] = 0.5 * (scalar + result)

    rate(load_scalar, range(1, 7), EXT, 0, keep_section)
    rate(load_section, range(2, 6), 32, 2, keep_result)


def call(kernel, outs, flops, limit, scratch=(), smem=0):
    vmem = pl.BlockSpec(memory_space=pltpu.VMEM)

    def run(*args):
        specs = [pl.BlockSpec(memory_space=pltpu.SMEM)] * smem + [vmem] * (len(args) - smem)
        size = sum(math.prod(a.shape) * a.dtype.itemsize for a in args)
        return pl.pallas_call(
            kernel,
            out_shape=outs,
            in_specs=specs,
            out_specs=jax.tree.map(lambda _: vmem, outs),
            scratch_shapes=scratch,
            compiler_params=pltpu.CompilerParams(vmem_limit_bytes=limit * 2**20),
            cost_estimate=pl.CostEstimate(flops=flops, bytes_accessed=size, transcendentals=0),
        )(*args)

    return run


def shards(velocity_modes, scalar, nest_shift):
    bh, bl = (jnp.asarray(a) for a in split_host(row_plane_matrix()))
    of = jax.ShapeDtypeStruct

    def ring(axis):
        count = lax.axis_size(axis)
        up = [(i, (i + 1) % count) for i in range(count)]
        return up, [(b, a) for a, b in up]

    def exchange(block):
        block = block.reshape(32, 16, 128)
        return lax.all_to_all(block, "wa", split_axis=0, concat_axis=0, tiled=True).reshape(512, 128)

    modes = velocity_modes.reshape(64, 512)
    seeds = jnp.asarray(cas_seeds())
    full = (pltpu.VMEM((N, N), BF16),) * 2
    retained = (pltpu.VMEM((N, 512), BF16),) * 2
    sent = call(synth_y_kernel, of((512, 128), F32), 10**9, 12, scratch=full)(modes, seeds)
    received = exchange(sent)

    up, down = ring("wa")
    before = lax.ppermute(scalar[:, 30:32, :].reshape(8, 1024), "wa", up)
    after = lax.ppermute(scalar[:, 0:2, :].reshape(8, 1024), "wa", down)

    payload = of((PAYLOAD, 128), F32)
    to_up, to_down = call(pack_kernel, (payload, payload), 10**6, 8)(
        received, scalar, before, after
    )
    up, down = ring("gz")
    from_low = lax.ppermute(to_up, "gz", up)
    from_high = lax.ppermute(to_down, "gz", down)

    spaced, half = call(
        spectral_kernel, (of((N, 128), F32), of((512, 128), F32)), 10**9, 12, scratch=full
    )(to_up, seeds)
    returned = exchange(half)

    scalar_next = call(
        fine_kernel,
        of((4, 32, 1024), F32),
        2 * 10**9,
        24,
        scratch=retained
        + (
            pltpu.VMEM((3, N + 128, 128), F32),
            pltpu.VMEM((2, 8, 6 * EXT, 128), F32),
            pltpu.VMEM((6 * 8 * EXT + 8, 128), F32),
        ),
        smem=1,
    )(nest_shift, spaced, to_up, to_down, from_low, from_high, seeds, bh, bl)

    stress = call(
        analysis_y_kernel, of((64, 512), BF16), 10**9, 8, scratch=retained
    )(returned, seeds)
    return (stress.reshape(2, 2, 16, 512), scalar_next)


def solution(mesh):
    placed = (P(None, "gz", "wa", None), P("gz", "wa", None), P())
    return jax.shard_map(
        shards,
        mesh=mesh,
        in_specs=placed,
        out_specs=(P(None, "gz", "wa", None), P("gz", "wa", None)),
        check_vma=False,
    )
```

```python
import math

import jax
import jax.numpy as jnp
import ml_dtypes
import numpy as np
from jax import lax
from jax.experimental import pallas as pl
from jax.experimental.pallas import tpu as pltpu
from jax.sharding import PartitionSpec as P


F32 = jnp.float32
BF16 = jnp.bfloat16
N = 768
HALF = 256
OWN = 24
ROWS = 32
EXT = 40
RETAINED = (0, 1, 4, 5)
BASE = 512
PAYLOAD = BASE + 2 * 8 * EXT + 8


def split_host(array):
    high = array.astype(np.float32).astype(ml_dtypes.bfloat16)
    low = (array - high.astype(np.float64)).astype(np.float32).astype(ml_dtypes.bfloat16)
    return high, low


def cas_seeds():
    lane = np.arange(128, dtype=np.int64)
    rows = []
    for steps in (8 * np.arange(96, dtype=np.int64), np.arange(8, dtype=np.int64)):
        angle = ((steps[:, None] * lane) % N).astype(np.float64) * (2.0 * math.pi / N)
        rows += [np.cos(angle), np.sin(angle)]
    return np.concatenate(rows).astype(np.float32)


def weights_of(t):
    return (
        (-(t**3) + 2 * t**2 - t) / 2,
        (3 * t**3 - 5 * t**2 + 2) / 2,
        (-3 * t**3 + 4 * t**2 + t) / 2,
        (t**3 - t**2) / 2,
    )


def row_plane_matrix():
    along_y = np.zeros((EXT, ROWS))
    for e in range(1, 35):
        numer = 3 * (2 * (e - 2) + 1)
        for offset, weight in zip(range(-1, 3), weights_of((numer % 8) / 8.0)):
            along_y[e, numer // 8 + offset + 2] += weight
    along_z = np.zeros((6, 6))
    for k in range(6):
        numer = 2 * (k - 1) - 1
        for offset, weight in zip(range(-1, 3), weights_of((numer % 4) / 4.0)):
            along_z[k, numer // 4 + offset + 2] += weight
    full = np.einsum("kp,er->kepr", along_z, along_y).reshape(6 * EXT, 6, ROWS)
    below, own, above = (full[:, i : i + 2].reshape(6 * EXT, 64) for i in (0, 2, 4))
    none = np.zeros_like(own)
    return np.stack(
        [
            np.concatenate([below, above, own, none], axis=1),
            np.concatenate([below, above, none, own], axis=1),
        ]
    )


def mm(a, b):
    return lax.dot_general(a, b, (((1,), (0,)), ((), ())), preferred_element_type=F32)


def mm_nt(a, b):
    return lax.dot_general(a, b, (((1,), (1,)), ((), ())), preferred_element_type=F32)


def split(x):
    high = x.astype(BF16)
    low = (x - high.astype(F32)).astype(BF16)
    return high, low


def lanes_of(shape):
    return lax.broadcasted_iota(jnp.int32, shape, len(shape) - 1)


def cos_sin(steps):
    centred = jnp.where(steps >= N // 2, steps - N, steps)
    quarter = centred.astype(F32) * (math.pi / (2 * N))
    square = quarter * quarter
    sin = cos = jnp.zeros_like(square)
    for i in range(5, -1, -1):
        sin = sin * square + (-1) ** i / math.factorial(2 * i + 1)
        cos = cos * square + (-1) ** i / math.factorial(2 * i)
    sin = sin * quarter
    for _ in range(2):
        sin, cos = 2.0 * sin * cos, 1.0 - 2.0 * sin * sin
    return cos, sin


def make_seeds(seed_ref):
    for first, count, scale in ((0, 96, 8), (192, 8, 1)):
        row = lax.broadcasted_iota(jnp.int32, (count, 128), 0)
        cos, sin = cos_sin(lax.rem(scale * row * lanes_of((count, 128)), N))
        seed_ref[first : first + count, :] = cos
        seed_ref[first + count : first + 2 * count, :] = sin


def make_table(seed_ref, fh_ref, fl_ref, blocks=(0, 1, 2, 3, 4, 5)):
    near_cos, near_sin = seed_ref[192:200, :], seed_ref[200:208, :]
    sublane = lax.broadcasted_iota(jnp.int32, (8, 128), 0)
    turns = []
    for phase in range(3):
        turns.append([])
        for b in range(3):
            sixth = lax.rem(b * (2 * phase + sublane), 6)
            cos, sin = jnp.ones((8, 128), F32), jnp.zeros((8, 128), F32)
            for i in range(1, 6):
                angle = 2.0 * math.pi * i / 6
                cos = jnp.where(sixth == i, round(math.cos(angle), 6), cos)
                sin = jnp.where(sixth == i, 0.0 if i == 3 else math.sin(angle), sin)
            turns[-1].append((cos, sin))
    parity = jnp.bitwise_and(lax.broadcasted_iota(jnp.int32, (16, 128), 0), 1)
    sign = (1 - 2 * parity).astype(F32).astype(BF16)

    def six(step, carry):
        for pair in range(3):
            parts = ([], [], [])
            for i in (2 * pair, 2 * pair + 1):
                m = 6 * step + i
                far_cos, far_sin = seed_ref[pl.ds(m, 1), :], seed_ref[pl.ds(96 + m, 1), :]
                cos = far_cos * near_cos - far_sin * near_sin
                sin = far_sin * near_cos + far_cos * near_sin
                plus, minus = cos + sin, cos - sin
                parts[0].append(plus)
                for b in (1, 2):
                    turn_cos, turn_sin = turns[i % 3][b]
                    parts[b].append(turn_cos * plus + turn_sin * minus)
            halves = [split(jnp.concatenate(p, axis=0)) for p in parts]
            row = pl.multiple_of(48 * step + 16 * pair, 16)
            for place, b in enumerate(blocks):
                for ref, half in zip((fh_ref, fl_ref), halves[b % 3]):
                    ref[pl.ds(row, 16), 128 * place : 128 * place + 128] = (
                        half if b < 3 else half * sign
                    )
        return carry

    lax.fori_loop(0, 16, six, 0, unroll=4)


def synth_y_kernel(m_hbm, out_ref, fh_ref, fl_ref, seed_ref, m_ref, sem):
    modes_copy = pltpu.make_async_copy(m_hbm, m_ref, sem)
    modes_copy.start()
    make_seeds(seed_ref)
    make_table(seed_ref, fh_ref, fl_ref)
    modes_copy.wait()
    mh, ml = split(m_ref[...])
    both = jnp.concatenate([mh, ml], axis=0)
    stacked = mm(both[:, :HALF], fh_ref[0:HALF, :]) + mm(both[:, HALF:], fh_ref[512:, :])
    lines = stacked[:64] + stacked[64:]
    lines = lines + mm(mh[:, :HALF], fl_ref[0:HALF, :]) + mm(mh[:, HALF:], fl_ref[512:, :])
    tiles = [lines[:, 128 * t : 128 * t + 128] for t in range(6)]
    lane = lanes_of((64, 128))
    group = lanes_of((16, 128)) // 32
    for d in range(32):
        start = (OWN * d - 2) % N
        t, first = start // 128, start % 128
        window = tiles[t]
        if first + ROWS > 128:
            window = jnp.where(lane >= first, window, tiles[(t + 1) % 6])
        chunk = None
        for cz in range(4):
            piece = window[16 * cz : 16 * cz + 16]
            shift = (32 * cz - first) % 128
            if shift:
                piece = pltpu.roll(piece, shift, 1)
            chunk = piece if chunk is None else jnp.where(group == cz, piece, chunk)
        out_ref[16 * d : 16 * d + 16, :] = chunk


def pack_kernel(r_ref, g_ref, before_ref, after_ref, up_ref, down_ref):
    received = r_ref[...]
    for ref in (up_ref, down_ref):
        ref[0:BASE, :] = received
        ref[PAYLOAD - 8 : PAYLOAD, :] = jnp.zeros((8, 128), F32)
    for p in range(4):
        ref = down_ref if p < 2 else up_ref
        for t in range(8):
            row = BASE + ((p % 2) * 8 + t) * EXT
            columns = slice(128 * t, 128 * t + 128)
            ref[row : row + 2, :] = before_ref[2 * p : 2 * p + 2, columns]
            ref[row + 2 : row + 34, :] = g_ref[p, :, columns]
            ref[row + 34 : row + 36, :] = after_ref[2 * p : 2 * p + 2, columns]
            ref[row + 36 : row + 40, :] = jnp.zeros((4, 128), F32)


def spectral_kernel(r_ref, seed_ref, out_ref, fh_ref, fl_ref):
    make_table(seed_ref, fh_ref, fl_ref)
    rh, rl = split(r_ref[0:BASE, :])
    both = jnp.concatenate([rh, rl], axis=1)
    o = mm(fh_ref[:, 0:HALF], both[0:HALF]) + mm(fh_ref[:, 512:], both[HALF:])
    spaced = o[:, :128] + o[:, 128:]
    spaced = spaced + mm(fl_ref[:, 0:HALF], rh[0:HALF]) + mm(fl_ref[:, 512:], rh[HALF:])
    swapped = pltpu.roll(spaced, 64, 1)
    products = jnp.where(
        lanes_of((N, 128)) < 64,
        spaced * spaced - swapped * swapped,
        spaced * swapped,
    )
    ph, plo = split(products)
    both = jnp.concatenate([ph, plo], axis=1)
    for first, row in ((0, 0), (512, HALF)):
        o = mm(fh_ref[first : first + HALF, :], both)
        out_ref[row : row + HALF, :] = (
            o[:, :128] + o[:, 128:] + mm(fl_ref[first : first + HALF, :], ph)
        )


def analysis_y_kernel(r_ref, seed_ref, out_ref, fh_ref, fl_ref):
    make_table(seed_ref, fh_ref, fl_ref, RETAINED)
    lane = lanes_of((16, 128))
    columns = []
    for t in range(6):
        rows = []
        for cz in range(4):
            tile = None
            for d in range(32):
                low, high = OWN * d - 128 * t, OWN * d - 128 * t + OWN
                if high <= 0 or low >= 128:
                    continue
                shift = (low - (32 * cz + 2)) % 128
                piece = r_ref[16 * d : 16 * d + 16, :]
                if shift:
                    piece = pltpu.roll(piece, shift, 1)
                tile = piece if tile is None else jnp.where(lane >= low, piece, tile)
            rows.append(tile)
        columns.append(jnp.concatenate(rows, axis=0))
    lines = jnp.concatenate(columns, axis=1)
    ah, al = split(lines)
    both = jnp.concatenate([ah, al], axis=0)
    o = mm(both, fh_ref[...])
    o = o[:64] + o[64:] + mm(ah, fl_ref[...])
    out_ref[...] = (o * (1.0 / N)).astype(BF16)


def flux(g, gg, h):
    return (h - g) * (gg + h * h)


def fine_kernel(
    shift_ref,
    up_ref,
    down_ref,
    low_ref,
    high_ref,
    seed_ref,
    b_ref,
    out_ref,
    fh_ref,
    fl_ref,
    x_ref,
    u_ref,
    s_ref,
):
    make_table(seed_ref, fh_ref, fl_ref, RETAINED)
    below = low_ref[0:BASE, :]
    above = high_ref[0:BASE, :]
    left = lanes_of((BASE, 128)) < 64
    first = jnp.where(left, below, pltpu.roll(above, 64, 1))
    second = jnp.where(left, pltpu.roll(below, 64, 1), above)
    rh, rl = split(jnp.concatenate([first, second, up_ref[0:BASE, :]], axis=1))
    halo = mm(fh_ref[...], rh) + mm(fh_ref[...], rl) + mm(fl_ref[...], rh)
    for i in range(3):
        tile = halo[:, 128 * i : 128 * i + 128]
        x_ref[i, 0:N, :] = tile
        x_ref[i, N : N + 128, :] = tile[0:128]

    shift = shift_ref[0]
    base = lax.shift_right_arithmetic(3 * (1 + 2 * shift), 3) - 1
    cell = lax.broadcasted_iota(jnp.int32, (128, 128), 0)
    coarse = lanes_of((128, 128))
    numer = 3 * (2 * cell + 1 + 2 * shift)
    lower = lax.shift_right_arithmetic(numer, 3) - base
    t = jnp.bitwise_and(numer, 7).astype(F32) * 0.125
    square = t * t
    cube = square * t
    weights = (
        (-cube + 2.0 * square - t) * 0.5,
        (3.0 * cube - 5.0 * square + 2.0) * 0.5,
        (-3.0 * cube + 4.0 * square + t) * 0.5,
        (cube - square) * 0.5,
    )
    matrix = jnp.zeros((128, 128), F32)
    for offset, weight in zip(range(-1, 3), weights):
        matrix = matrix + jnp.where(coarse == lower + offset, weight, 0.0)
    wh, wl = split(matrix)
    both = jnp.concatenate([wh, wl], axis=0)

    for pair in range(4):
        lines = []
        for b in (2 * pair, 2 * pair + 1):
            start = lax.rem(base + N + 96 * b, N)
            window = jnp.concatenate([x_ref[i, pl.ds(start, 128), :] for i in range(3)], axis=1)
            vh, vl = split(window)
            o = mm(both, vh)
            lines.append(o[:128] + o[128:] + mm(wh, vl))
        lines = jnp.concatenate(lines, axis=0)
        for c in range(2):
            mine = jnp.concatenate([lines[:, 128 * c : 128 * c + 128], lines[:, 256:]], axis=1)
            vh, vl = split(mine)
            o = mm_nt(b_ref[c], vh)
            o = o[:240] + o[240:] + mm_nt(b_ref[c, 0:240, :], vl)
            u_ref[c, 2 * pair] = o[:, :128]
            u_ref[c, 2 * pair + 1] = o[:, 128:]

    homes = ((low_ref, 0), (low_ref, 1), (down_ref, 0), (down_ref, 1))
    homes = homes + ((up_ref, 0), (up_ref, 1), (high_ref, 0), (high_ref, 1))

    def around(centre, west, east):
        lane = lanes_of(centre.shape)
        to_east = pltpu.roll(jnp.where(lane == 0, east, centre), 127, 1)
        to_west = pltpu.roll(jnp.where(lane == 127, west, centre), 1, 1)
        return to_west, to_east

    def rate(load, planes, count, skip, use):
        def one(t, carry):
            west_t = lax.rem(t + 7, 8)
            east_t = lax.rem(t + 1, 8)
            first = planes[0]
            g = load(first, t, skip, count)
            gg = 2.0 + g * g
            below = load(first - 1, t, skip, count)
            lower = -flux(g, gg, below)
            for p in planes:
                above = load(p + 1, t, skip, count)
                north = load(p, t, skip + 1, count)
                south = load(p, t, skip - 1, count)
                west, east = around(
                    g, load(p, west_t, skip, count), load(p, east_t, skip, count)
                )
                row = (p - 1) * EXT + skip
                total = u_ref[0, t, row : row + count, :] * (east - west)
                total = total + u_ref[1, t, row : row + count, :] * (north - south)
                total = total + flux(g, gg, north) + flux(g, gg, south)
                total = total + flux(g, gg, east) + flux(g, gg, west)
                square = above * above
                upper = (above - g) * (gg + square)
                total = total + upper - lower
                use(p, t, g, g + 0.01 * total)
                lower, g, gg = upper, above, 2.0 + square
            return carry

        lax.fori_loop(0, 8, one, 0, unroll=2)

    def load_scalar(p, t, skip, count):
        ref, plane = homes[p]
        row = pl.multiple_of(BASE + (plane * 8 + t) * EXT, 8)
        return ref[pl.ds(row + skip, count), :]

    def load_section(p, t, skip, count):
        row = pl.multiple_of(((p - 1) * 8 + t) * EXT, 8)
        return s_ref[pl.ds(row + skip, count), :]

    def keep_section(p, t, g, result):
        row = pl.multiple_of(((p - 1) * 8 + t) * EXT, 8)
        s_ref[pl.ds(row, EXT), :] = result

    def keep_result(p, t, g, result):
        scalar = load_scalar(p, t, 2, 32)
        column = pl.multiple_of(t * 128, 128)
        out_ref[p - 2, :, pl.ds(column, 128)] = 0.5 * (scalar + result)

    rate(load_scalar, range(1, 7), EXT, 0, keep_section)
    rate(load_section, range(2, 6), 32, 2, keep_result)


def call(kernel, outs, flops, limit, scratch=(), smem=0, home=pltpu.VMEM):
    vmem = pl.BlockSpec(memory_space=pltpu.VMEM)
    place = pl.BlockSpec(memory_space=home)

    def run(*args):
        specs = [pl.BlockSpec(memory_space=pltpu.SMEM)] * smem + [place] * (len(args) - smem)
        size = sum(math.prod(a.shape) * a.dtype.itemsize for a in args)
        return pl.pallas_call(
            kernel,
            out_shape=outs,
            in_specs=specs,
            out_specs=jax.tree.map(lambda _: vmem, outs),
            scratch_shapes=scratch,
            compiler_params=pltpu.CompilerParams(vmem_limit_bytes=limit * 2**20),
            cost_estimate=pl.CostEstimate(flops=flops, bytes_accessed=size, transcendentals=0),
        )(*args)

    return run


def shards(velocity_modes, scalar, nest_shift):
    stencil = jnp.asarray(np.concatenate(split_host(-10.0 * row_plane_matrix()), axis=1))
    of = jax.ShapeDtypeStruct

    def ring(axis):
        count = lax.axis_size(axis)
        up = [(i, (i + 1) % count) for i in range(count)]
        return up, [(b, a) for a, b in up]

    def exchange(block):
        block = block.reshape(32, 16, 128)
        return lax.all_to_all(block, "wa", split_axis=0, concat_axis=0, tiled=True).reshape(512, 128)

    modes = velocity_modes.reshape(64, 512)
    seeds = jnp.asarray(cas_seeds())
    full = (pltpu.VMEM((N, N), BF16),) * 2
    retained = (pltpu.VMEM((N, 512), BF16),) * 2
    sent = call(
        synth_y_kernel,
        of((512, 128), F32),
        10**9,
        60,
        scratch=full
        + (
            pltpu.VMEM((208, 128), F32),
            pltpu.VMEM((64, 512), F32),
            pltpu.SemaphoreType.DMA(()),
        ),
        home=pltpu.HBM,
    )(modes)
    received = exchange(sent)

    up, down = ring("wa")
    before = lax.ppermute(scalar[:, 30:32, :].reshape(8, 1024), "wa", up)
    after = lax.ppermute(scalar[:, 0:2, :].reshape(8, 1024), "wa", down)

    payload = of((PAYLOAD, 128), F32)
    to_up, to_down = call(pack_kernel, (payload, payload), 10**6, 8)(
        received, scalar, before, after
    )
    up, down = ring("gz")
    from_low = lax.ppermute(to_up, "gz", up)
    from_high = lax.ppermute(to_down, "gz", down)

    half = call(spectral_kernel, of((512, 128), F32), 10**9, 12, scratch=full)(to_up, seeds)
    returned = exchange(half)

    scalar_next = call(
        fine_kernel,
        of((4, 32, 1024), F32),
        2 * 10**9,
        24,
        scratch=retained
        + (
            pltpu.VMEM((3, N + 128, 128), F32),
            pltpu.VMEM((2, 8, 6 * EXT, 128), F32),
            pltpu.VMEM((6 * 8 * EXT + 8, 128), F32),
        ),
        smem=1,
    )(nest_shift, to_up, to_down, from_low, from_high, seeds, stencil)

    stress = call(
        analysis_y_kernel, of((64, 512), BF16), 10**9, 8, scratch=retained
    )(returned, seeds)
    return (stress.reshape(2, 2, 16, 512), scalar_next)


def solution(mesh):
    placed = (P(None, "gz", "wa", None), P("gz", "wa", None), P())
    return jax.shard_map(
        shards,
        mesh=mesh,
        in_specs=placed,
        out_specs=(P(None, "gz", "wa", None), P("gz", "wa", None)),
        check_vma=False,
    )
```

```python
import math

import jax
import jax.numpy as jnp
import ml_dtypes
import numpy as np
from jax import lax
from jax.experimental import pallas as pl
from jax.experimental.pallas import tpu as pltpu
from jax.sharding import PartitionSpec as P


F32 = jnp.float32
BF16 = jnp.bfloat16
N = 768
HALF = 256
OWN = 24
ROWS = 32
EXT = 40
BASE = 512
PAYLOAD = BASE + 2 * 8 * EXT + 8


def split_host(array):
    high = array.astype(np.float32).astype(ml_dtypes.bfloat16)
    low = (array - high.astype(np.float64)).astype(np.float32).astype(ml_dtypes.bfloat16)
    return high, low


def cas_seeds():
    lane = np.arange(128, dtype=np.int64)
    rows = []
    for steps in (8 * np.arange(96, dtype=np.int64), np.arange(8, dtype=np.int64)):
        angle = ((steps[:, None] * lane) % N).astype(np.float64) * (2.0 * math.pi / N)
        rows += [np.cos(angle), np.sin(angle)]
    return np.concatenate(rows).astype(np.float32)


def weights_of(t):
    return (
        (-(t**3) + 2 * t**2 - t) / 2,
        (3 * t**3 - 5 * t**2 + 2) / 2,
        (-3 * t**3 + 4 * t**2 + t) / 2,
        (t**3 - t**2) / 2,
    )


def row_plane_matrix():
    along_y = np.zeros((EXT, ROWS))
    for e in range(1, 35):
        numer = 3 * (2 * (e - 2) + 1)
        for offset, weight in zip(range(-1, 3), weights_of((numer % 8) / 8.0)):
            along_y[e, numer // 8 + offset + 2] += weight
    along_z = np.zeros((6, 6))
    for k in range(6):
        numer = 2 * (k - 1) - 1
        for offset, weight in zip(range(-1, 3), weights_of((numer % 4) / 4.0)):
            along_z[k, numer // 4 + offset + 2] += weight
    full = np.einsum("kp,er->kepr", along_z, along_y).reshape(6 * EXT, 6, ROWS)
    below, own, above = (full[:, i : i + 2].reshape(6 * EXT, 64) for i in (0, 2, 4))
    none = np.zeros_like(own)
    return np.stack(
        [
            np.concatenate([below, above, own, none], axis=1),
            np.concatenate([below, above, none, own], axis=1),
        ]
    )


def mm(a, b):
    return lax.dot_general(a, b, (((1,), (0,)), ((), ())), preferred_element_type=F32)


def mm_nt(a, b):
    return lax.dot_general(a, b, (((1,), (1,)), ((), ())), preferred_element_type=F32)


def split(x):
    high = x.astype(BF16)
    low = (x - high.astype(F32)).astype(BF16)
    return high, low


def lanes_of(shape):
    return lax.broadcasted_iota(jnp.int32, shape, len(shape) - 1)


def cos_sin(steps):
    centred = jnp.where(steps >= N // 2, steps - N, steps)
    quarter = centred.astype(F32) * (math.pi / (2 * N))
    square = quarter * quarter
    sin = cos = jnp.zeros_like(square)
    for i in range(5, -1, -1):
        sin = sin * square + (-1) ** i / math.factorial(2 * i + 1)
        cos = cos * square + (-1) ** i / math.factorial(2 * i)
    sin = sin * quarter
    for _ in range(2):
        sin, cos = 2.0 * sin * cos, 1.0 - 2.0 * sin * sin
    return cos, sin


def make_seeds(seed_ref):
    for first, count, scale in ((0, 96, 8), (192, 8, 1)):
        row = lax.broadcasted_iota(jnp.int32, (count, 128), 0)
        cos, sin = cos_sin(lax.rem(scale * row * lanes_of((count, 128)), N))
        seed_ref[first : first + count, :] = cos
        seed_ref[first + count : first + 2 * count, :] = sin


def sign_of(shape, dimension):
    return (1 - 2 * jnp.bitwise_and(lax.broadcasted_iota(jnp.int32, shape, dimension), 1)).astype(F32)


def three(fh, fl, high, low):
    return mm(fh, high) + mm(fh, low) + mm(fl, high)


def synth_x(fh_ref, fl_ref, lines):
    high, low = split(jnp.concatenate([lines, lines * sign_of(lines.shape, 0)], axis=1))
    plus = three(fh_ref[:, :HALF], fl_ref[:, :HALF], high[:HALF], low[:HALF])
    minus = three(fh_ref[:, 128:], fl_ref[:, 128:], high[HALF:], low[HALF:])
    return plus + sign_of(minus.shape, 0) * minus


def make_table(seed_ref, fh_ref, fl_ref):
    near_cos, near_sin = seed_ref[192:200, :], seed_ref[200:208, :]
    sublane = lax.broadcasted_iota(jnp.int32, (8, 128), 0)
    turns = []
    for phase in range(3):
        turns.append([])
        for b in range(3):
            sixth = lax.rem(b * (2 * phase + sublane), 6)
            cos, sin = jnp.ones((8, 128), F32), jnp.zeros((8, 128), F32)
            for i in range(1, 6):
                angle = 2.0 * math.pi * i / 6
                cos = jnp.where(sixth == i, round(math.cos(angle), 6), cos)
                sin = jnp.where(sixth == i, 0.0 if i == 3 else math.sin(angle), sin)
            turns[-1].append((cos, sin))

    def six(step, carry):
        for pair in range(3):
            parts = ([], [], [])
            for i in (2 * pair, 2 * pair + 1):
                m = 6 * step + i
                far_cos, far_sin = seed_ref[pl.ds(m, 1), :], seed_ref[pl.ds(96 + m, 1), :]
                cos = far_cos * near_cos - far_sin * near_sin
                sin = far_sin * near_cos + far_cos * near_sin
                plus, minus = cos + sin, cos - sin
                parts[0].append(plus)
                for b in (1, 2):
                    turn_cos, turn_sin = turns[i % 3][b]
                    parts[b].append(turn_cos * plus + turn_sin * minus)
            halves = [split(jnp.concatenate(p, axis=0)) for p in parts]
            row = pl.multiple_of(48 * step + 16 * pair, 16)
            for b in range(3):
                for ref, half in zip((fh_ref, fl_ref), halves[b]):
                    ref[pl.ds(row, 16), 128 * b : 128 * b + 128] = half
        return carry

    lax.fori_loop(0, 8, six, 0, unroll=4)


def synth_y_kernel(m_hbm, out_ref, fh_ref, fl_ref, seed_ref, m_ref, sem):
    modes_copy = pltpu.make_async_copy(m_hbm, m_ref, sem)
    modes_copy.start()
    make_seeds(seed_ref)
    make_table(seed_ref, fh_ref, fl_ref)
    modes_copy.wait()
    modes = m_ref[...]
    mh, ml = split(modes)
    nh, nl = split(modes * sign_of(modes.shape, 1))
    both = jnp.concatenate([mh, ml, nh, nl], axis=0)
    high = jnp.concatenate([mh, nh], axis=0)
    o = mm(both[:, HALF:], fh_ref[128:, :])
    o = mm(both[:, :HALF], fh_ref[:HALF, :]) + sign_of(o.shape, 1) * o
    p = mm(high[:, HALF:], fl_ref[128:, :])
    p = mm(high[:, :HALF], fl_ref[:HALF, :]) + sign_of(p.shape, 1) * p
    first = o[0:64] + o[64:128] + p[0:64]
    second = o[128:192] + o[192:256] + p[64:128]
    lines = jnp.concatenate([first, second], axis=1)
    tiles = [lines[:, 128 * t : 128 * t + 128] for t in range(6)]
    lane = lanes_of((64, 128))
    group = lanes_of((16, 128)) // 32
    for d in range(32):
        start = (OWN * d - 2) % N
        t, first = start // 128, start % 128
        window = tiles[t]
        if first + ROWS > 128:
            window = jnp.where(lane >= first, window, tiles[(t + 1) % 6])
        chunk = None
        for cz in range(4):
            piece = window[16 * cz : 16 * cz + 16]
            shift = (32 * cz - first) % 128
            if shift:
                piece = pltpu.roll(piece, shift, 1)
            chunk = piece if chunk is None else jnp.where(group == cz, piece, chunk)
        out_ref[16 * d : 16 * d + 16, :] = chunk


def pack_kernel(r_ref, g_ref, before_ref, after_ref, up_ref, down_ref):
    received = r_ref[...]
    for ref in (up_ref, down_ref):
        ref[0:BASE, :] = received
        ref[PAYLOAD - 8 : PAYLOAD, :] = jnp.zeros((8, 128), F32)
    for p in range(4):
        ref = down_ref if p < 2 else up_ref
        for t in range(8):
            row = BASE + ((p % 2) * 8 + t) * EXT
            columns = slice(128 * t, 128 * t + 128)
            ref[row : row + 2, :] = before_ref[2 * p : 2 * p + 2, columns]
            ref[row + 2 : row + 34, :] = g_ref[p, :, columns]
            ref[row + 34 : row + 36, :] = after_ref[2 * p : 2 * p + 2, columns]
            ref[row + 36 : row + 40, :] = jnp.zeros((4, 128), F32)


def spectral_kernel(r_ref, seed_ref, out_ref, fh_ref, fl_ref):
    make_table(seed_ref, fh_ref, fl_ref)
    spaced = synth_x(fh_ref, fl_ref, r_ref[0:BASE, :])
    halves = []
    for half in (spaced[:, :128], spaced[:, 128:]):
        swapped = pltpu.roll(half, 64, 1)
        halves.append(
            jnp.where(
                lanes_of(half.shape) < 64, half * half - swapped * swapped, half * swapped
            )
        )
    products = jnp.concatenate(halves, axis=1)
    for first, row in ((0, 0), (128, HALF)):
        if row:
            products = products * sign_of(products.shape, 0)
        high, low = split(products)
        rows = slice(first, first + HALF)
        o = three(fh_ref[rows, :], fl_ref[rows, :], high, low)
        out_ref[row : row + HALF, :] = o[:, :128] + sign_of((HALF, 128), 0) * o[:, 128:]


def analysis_y_kernel(r_ref, seed_ref, out_ref, fh_ref, fl_ref):
    make_table(seed_ref, fh_ref, fl_ref)
    lane = lanes_of((16, 128))
    columns = []
    for t in range(6):
        rows = []
        for cz in range(4):
            tile = None
            for d in range(32):
                low, high = OWN * d - 128 * t, OWN * d - 128 * t + OWN
                if high <= 0 or low >= 128:
                    continue
                shift = (low - (32 * cz + 2)) % 128
                piece = r_ref[16 * d : 16 * d + 16, :]
                if shift:
                    piece = pltpu.roll(piece, shift, 1)
                tile = piece if tile is None else jnp.where(lane >= low, piece, tile)
            rows.append(tile)
        columns.append(jnp.concatenate(rows, axis=0))
    lines = jnp.concatenate(columns, axis=1)
    for first, column in ((0, 0), (128, HALF)):
        if column:
            lines = lines * sign_of(lines.shape, 1)
        high, low = split(lines)
        rows = [part[:, 384 * i : 384 * i + 384] for i in range(2) for part in (high, low)]
        o = mm(jnp.concatenate(rows, axis=0), fh_ref[:, first : first + HALF])
        p = mm(jnp.concatenate(rows[::2], axis=0), fl_ref[:, first : first + HALF])
        near = o[0:64] + o[64:128] + p[0:64]
        far = o[128:192] + o[192:256] + p[64:128]
        total = near + sign_of(far.shape, 1) * far
        out_ref[:, column : column + HALF] = (total * (1.0 / N)).astype(BF16)


def flux(g, gg, h):
    return (h - g) * (gg + h * h)


def fine_kernel(
    shift_ref,
    up_ref,
    down_ref,
    low_ref,
    high_ref,
    seed_ref,
    b_ref,
    out_ref,
    fh_ref,
    fl_ref,
    x_ref,
    u_ref,
    s_ref,
):
    make_table(seed_ref, fh_ref, fl_ref)
    below = low_ref[0:BASE, :]
    above = high_ref[0:BASE, :]
    left = lanes_of((BASE, 128)) < 64
    first = jnp.where(left, below, pltpu.roll(above, 64, 1))
    second = jnp.where(left, pltpu.roll(below, 64, 1), above)
    for i, lines in enumerate((first, second, up_ref[0:BASE, :])):
        points = synth_x(fh_ref, fl_ref, lines)
        x_ref[i, 0:384, :] = points[:, :128]
        x_ref[i, 384:N, :] = points[:, 128:]
        x_ref[i, N : N + 128, :] = points[0:128, :128]

    shift = shift_ref[0]
    base = lax.shift_right_arithmetic(3 * (1 + 2 * shift), 3) - 1
    cell = lax.broadcasted_iota(jnp.int32, (128, 128), 0)
    coarse = lanes_of((128, 128))
    numer = 3 * (2 * cell + 1 + 2 * shift)
    lower = lax.shift_right_arithmetic(numer, 3) - base
    t = jnp.bitwise_and(numer, 7).astype(F32) * 0.125
    square = t * t
    cube = square * t
    weights = (
        (-cube + 2.0 * square - t) * 0.5,
        (3.0 * cube - 5.0 * square + 2.0) * 0.5,
        (-3.0 * cube + 4.0 * square + t) * 0.5,
        (cube - square) * 0.5,
    )
    matrix = jnp.zeros((128, 128), F32)
    for offset, weight in zip(range(-1, 3), weights):
        matrix = matrix + jnp.where(coarse == lower + offset, weight, 0.0)
    wh, wl = split(matrix)
    both = jnp.concatenate([wh, wl], axis=0)

    for pair in range(4):
        lines = []
        for b in (2 * pair, 2 * pair + 1):
            start = lax.rem(base + N + 96 * b, N)
            window = jnp.concatenate([x_ref[i, pl.ds(start, 128), :] for i in range(3)], axis=1)
            vh, vl = split(window)
            o = mm(both, vh)
            lines.append(o[:128] + o[128:] + mm(wh, vl))
        lines = jnp.concatenate(lines, axis=0)
        for c in range(2):
            mine = jnp.concatenate([lines[:, 128 * c : 128 * c + 128], lines[:, 256:]], axis=1)
            vh, vl = split(mine)
            o = mm_nt(b_ref[c], vh)
            o = o[:240] + o[240:] + mm_nt(b_ref[c, 0:240, :], vl)
            u_ref[c, 2 * pair] = o[:, :128]
            u_ref[c, 2 * pair + 1] = o[:, 128:]

    homes = ((low_ref, 0), (low_ref, 1), (down_ref, 0), (down_ref, 1))
    homes = homes + ((up_ref, 0), (up_ref, 1), (high_ref, 0), (high_ref, 1))

    def around(centre, west, east):
        lane = lanes_of(centre.shape)
        to_east = pltpu.roll(jnp.where(lane == 0, east, centre), 127, 1)
        to_west = pltpu.roll(jnp.where(lane == 127, west, centre), 1, 1)
        return to_west, to_east

    def rate(load, planes, count, skip, use):
        def one(t, carry):
            west_t = lax.rem(t + 7, 8)
            east_t = lax.rem(t + 1, 8)
            first = planes[0]
            g = load(first, t, skip, count)
            gg = 2.0 + g * g
            below = load(first - 1, t, skip, count)
            lower = -flux(g, gg, below)
            for p in planes:
                above = load(p + 1, t, skip, count)
                north = load(p, t, skip + 1, count)
                south = load(p, t, skip - 1, count)
                west, east = around(
                    g, load(p, west_t, skip, count), load(p, east_t, skip, count)
                )
                row = (p - 1) * EXT + skip
                total = u_ref[0, t, row : row + count, :] * (east - west)
                total = total + u_ref[1, t, row : row + count, :] * (north - south)
                total = total + flux(g, gg, north) + flux(g, gg, south)
                total = total + flux(g, gg, east) + flux(g, gg, west)
                square = above * above
                upper = (above - g) * (gg + square)
                total = total + upper - lower
                use(p, t, g, g + 0.01 * total)
                lower, g, gg = upper, above, 2.0 + square
            return carry

        lax.fori_loop(0, 8, one, 0, unroll=2)

    def load_scalar(p, t, skip, count):
        ref, plane = homes[p]
        row = pl.multiple_of(BASE + (plane * 8 + t) * EXT, 8)
        return ref[pl.ds(row + skip, count), :]

    def load_section(p, t, skip, count):
        row = pl.multiple_of(((p - 1) * 8 + t) * EXT, 8)
        return s_ref[pl.ds(row + skip, count), :]

    def keep_section(p, t, g, result):
        row = pl.multiple_of(((p - 1) * 8 + t) * EXT, 8)
        s_ref[pl.ds(row, EXT), :] = result

    def keep_result(p, t, g, result):
        scalar = load_scalar(p, t, 2, 32)
        column = pl.multiple_of(t * 128, 128)
        out_ref[p - 2, :, pl.ds(column, 128)] = 0.5 * (scalar + result)

    rate(load_scalar, range(1, 7), EXT, 0, keep_section)
    rate(load_section, range(2, 6), 32, 2, keep_result)


def call(kernel, outs, flops, limit, scratch=(), smem=0, home=pltpu.VMEM):
    vmem = pl.BlockSpec(memory_space=pltpu.VMEM)
    place = pl.BlockSpec(memory_space=home)

    def run(*args):
        specs = [pl.BlockSpec(memory_space=pltpu.SMEM)] * smem + [place] * (len(args) - smem)
        size = sum(math.prod(a.shape) * a.dtype.itemsize for a in args)
        return pl.pallas_call(
            kernel,
            out_shape=outs,
            in_specs=specs,
            out_specs=jax.tree.map(lambda _: vmem, outs),
            scratch_shapes=scratch,
            compiler_params=pltpu.CompilerParams(vmem_limit_bytes=limit * 2**20),
            cost_estimate=pl.CostEstimate(flops=flops, bytes_accessed=size, transcendentals=0),
        )(*args)

    return run


def shards(velocity_modes, scalar, nest_shift):
    stencil = jnp.asarray(np.concatenate(split_host(-10.0 * row_plane_matrix()), axis=1))
    of = jax.ShapeDtypeStruct

    def ring(axis):
        count = lax.axis_size(axis)
        up = [(i, (i + 1) % count) for i in range(count)]
        return up, [(b, a) for a, b in up]

    def exchange(block):
        block = block.reshape(32, 16, 128)
        return lax.all_to_all(block, "wa", split_axis=0, concat_axis=0, tiled=True).reshape(512, 128)

    modes = velocity_modes.reshape(64, 512)
    seeds = jnp.asarray(cas_seeds())
    table = (pltpu.VMEM((N // 2, N // 2), BF16),) * 2
    sent = call(
        synth_y_kernel,
        of((512, 128), F32),
        10**9,
        60,
        scratch=table
        + (
            pltpu.VMEM((208, 128), F32),
            pltpu.VMEM((64, 512), F32),
            pltpu.SemaphoreType.DMA(()),
        ),
        home=pltpu.HBM,
    )(modes)
    received = exchange(sent)

    up, down = ring("wa")
    before = lax.ppermute(scalar[:, 30:32, :].reshape(8, 1024), "wa", up)
    after = lax.ppermute(scalar[:, 0:2, :].reshape(8, 1024), "wa", down)

    payload = of((PAYLOAD, 128), F32)
    to_up, to_down = call(pack_kernel, (payload, payload), 10**6, 8)(
        received, scalar, before, after
    )
    up, down = ring("gz")
    from_low = lax.ppermute(to_up, "gz", up)
    from_high = lax.ppermute(to_down, "gz", down)

    half = call(spectral_kernel, of((512, 128), F32), 10**9, 12, scratch=table)(to_up, seeds)
    returned = exchange(half)

    scalar_next = call(
        fine_kernel,
        of((4, 32, 1024), F32),
        2 * 10**9,
        24,
        scratch=table
        + (
            pltpu.VMEM((3, N + 128, 128), F32),
            pltpu.VMEM((2, 8, 6 * EXT, 128), F32),
            pltpu.VMEM((6 * 8 * EXT + 8, 128), F32),
        ),
        smem=1,
    )(nest_shift, to_up, to_down, from_low, from_high, seeds, stencil)

    stress = call(analysis_y_kernel, of((64, 512), BF16), 10**9, 8, scratch=table)(returned, seeds)
    return (stress.reshape(2, 2, 16, 512), scalar_next)


def solution(mesh):
    placed = (P(None, "gz", "wa", None), P("gz", "wa", None), P())
    return jax.shard_map(
        shards,
        mesh=mesh,
        in_specs=placed,
        out_specs=(P(None, "gz", "wa", None), P("gz", "wa", None)),
        check_vma=False,
    )
```

```python
import math

import jax
import jax.numpy as jnp
import ml_dtypes
import numpy as np
from jax import lax
from jax.experimental import pallas as pl
from jax.experimental.pallas import tpu as pltpu
from jax.sharding import PartitionSpec as P


F32 = jnp.float32
BF16 = jnp.bfloat16
N = 768
HALF = 256
OWN = 24
ROWS = 32
EXT = 40
BASE = 512
PAYLOAD = BASE + 2 * 8 * EXT + 8


def split_host(array):
    high = array.astype(np.float32).astype(ml_dtypes.bfloat16)
    low = (array - high.astype(np.float64)).astype(np.float32).astype(ml_dtypes.bfloat16)
    return high, low


def cas_seeds():
    lane = np.arange(128, dtype=np.int64)
    rows = []
    for steps in (8 * np.arange(96, dtype=np.int64), np.arange(8, dtype=np.int64)):
        angle = ((steps[:, None] * lane) % N).astype(np.float64) * (2.0 * math.pi / N)
        rows += [np.cos(angle), np.sin(angle)]
    return np.concatenate(rows).astype(np.float32)


def weights_of(t):
    return (
        (-(t**3) + 2 * t**2 - t) / 2,
        (3 * t**3 - 5 * t**2 + 2) / 2,
        (-3 * t**3 + 4 * t**2 + t) / 2,
        (t**3 - t**2) / 2,
    )


def row_plane_matrix():
    along_y = np.zeros((EXT, ROWS))
    for e in range(1, 35):
        numer = 3 * (2 * (e - 2) + 1)
        for offset, weight in zip(range(-1, 3), weights_of((numer % 8) / 8.0)):
            along_y[e, numer // 8 + offset + 2] += weight
    along_z = np.zeros((6, 6))
    for k in range(6):
        numer = 2 * (k - 1) - 1
        for offset, weight in zip(range(-1, 3), weights_of((numer % 4) / 4.0)):
            along_z[k, numer // 4 + offset + 2] += weight
    full = np.einsum("kp,er->kepr", along_z, along_y).reshape(6 * EXT, 6, ROWS)
    below, own, above = (full[:, i : i + 2].reshape(6 * EXT, 64) for i in (0, 2, 4))
    none = np.zeros_like(own)
    return np.stack(
        [
            np.concatenate([below, above, own, none], axis=1),
            np.concatenate([below, above, none, own], axis=1),
        ]
    )


def mm(a, b):
    return lax.dot_general(a, b, (((1,), (0,)), ((), ())), preferred_element_type=F32)


def mm_nt(a, b):
    return lax.dot_general(a, b, (((1,), (1,)), ((), ())), preferred_element_type=F32)


def split(x):
    high = x.astype(BF16)
    low = (x - high.astype(F32)).astype(BF16)
    return high, low


def lanes_of(shape):
    return lax.broadcasted_iota(jnp.int32, shape, len(shape) - 1)


def cos_sin(steps):
    centred = jnp.where(steps >= N // 2, steps - N, steps)
    quarter = centred.astype(F32) * (math.pi / (2 * N))
    square = quarter * quarter
    sin = cos = jnp.zeros_like(square)
    for i in range(5, -1, -1):
        sin = sin * square + (-1) ** i / math.factorial(2 * i + 1)
        cos = cos * square + (-1) ** i / math.factorial(2 * i)
    sin = sin * quarter
    for _ in range(2):
        sin, cos = 2.0 * sin * cos, 1.0 - 2.0 * sin * sin
    return cos, sin


def make_seeds(seed_ref):
    for first, count, scale in ((0, 96, 8), (192, 8, 1)):
        row = lax.broadcasted_iota(jnp.int32, (count, 128), 0)
        cos, sin = cos_sin(lax.rem(scale * row * lanes_of((count, 128)), N))
        seed_ref[first : first + count, :] = cos
        seed_ref[first + count : first + 2 * count, :] = sin


def sign_of(shape, dimension):
    return (1 - 2 * jnp.bitwise_and(lax.broadcasted_iota(jnp.int32, shape, dimension), 1)).astype(F32)


def three(fh, fl, high, low):
    return mm(fh, high) + mm(fh, low) + mm(fl, high)


def synth_x(fh_ref, fl_ref, lines):
    high, low = split(jnp.concatenate([lines, lines * sign_of(lines.shape, 0)], axis=1))
    plus = three(fh_ref[:, :HALF], fl_ref[:, :HALF], high[:HALF], low[:HALF])
    minus = three(fh_ref[:, 128:], fl_ref[:, 128:], high[HALF:], low[HALF:])
    return plus + sign_of(minus.shape, 0) * minus


def make_table(seed_ref, fh_ref, fl_ref):
    near_cos, near_sin = seed_ref[192:200, :], seed_ref[200:208, :]
    sublane = lax.broadcasted_iota(jnp.int32, (8, 128), 0)
    turns = []
    for phase in range(3):
        turns.append([])
        for b in range(3):
            sixth = lax.rem(b * (2 * phase + sublane), 6)
            cos, sin = jnp.ones((8, 128), F32), jnp.zeros((8, 128), F32)
            for i in range(1, 6):
                angle = 2.0 * math.pi * i / 6
                cos = jnp.where(sixth == i, round(math.cos(angle), 6), cos)
                sin = jnp.where(sixth == i, 0.0 if i == 3 else math.sin(angle), sin)
            turns[-1].append((cos, sin))

    def six(step, carry):
        for pair in range(3):
            parts = ([], [], [])
            for i in (2 * pair, 2 * pair + 1):
                m = 6 * step + i
                far_cos, far_sin = seed_ref[pl.ds(m, 1), :], seed_ref[pl.ds(96 + m, 1), :]
                cos = far_cos * near_cos - far_sin * near_sin
                sin = far_sin * near_cos + far_cos * near_sin
                plus, minus = cos + sin, cos - sin
                parts[0].append(plus)
                for b in (1, 2):
                    turn_cos, turn_sin = turns[i % 3][b]
                    parts[b].append(turn_cos * plus + turn_sin * minus)
            halves = [split(jnp.concatenate(p, axis=0)) for p in parts]
            row = pl.multiple_of(48 * step + 16 * pair, 16)
            for b in range(3):
                for ref, half in zip((fh_ref, fl_ref), halves[b]):
                    ref[pl.ds(row, 16), 128 * b : 128 * b + 128] = half
        return carry

    lax.fori_loop(0, 8, six, 0, unroll=4)


def synth_y_kernel(m_hbm, out_ref, fh_ref, fl_ref, seed_ref, m_ref, sem):
    modes_copy = pltpu.make_async_copy(m_hbm, m_ref, sem)
    modes_copy.start()
    make_seeds(seed_ref)
    make_table(seed_ref, fh_ref, fl_ref)
    modes_copy.wait()
    modes = m_ref[...]
    mh, ml = split(modes)
    nh, nl = split(modes * sign_of(modes.shape, 1))
    both = jnp.concatenate([mh, ml, nh, nl], axis=0)
    high = jnp.concatenate([mh, nh], axis=0)
    o = mm(both[:, HALF:], fh_ref[128:, :])
    o = mm(both[:, :HALF], fh_ref[:HALF, :]) + sign_of(o.shape, 1) * o
    p = mm(high[:, HALF:], fl_ref[128:, :])
    p = mm(high[:, :HALF], fl_ref[:HALF, :]) + sign_of(p.shape, 1) * p
    first = o[0:64] + o[64:128] + p[0:64]
    second = o[128:192] + o[192:256] + p[64:128]
    lines = jnp.concatenate([first, second], axis=1)
    tiles = [lines[:, 128 * t : 128 * t + 128] for t in range(6)]
    lane = lanes_of((64, 128))
    group = lanes_of((16, 128)) // 32
    for d in range(32):
        start = (OWN * d - 2) % N
        t, first = start // 128, start % 128
        window = tiles[t]
        if first + ROWS > 128:
            window = jnp.where(lane >= first, window, tiles[(t + 1) % 6])
        chunk = None
        for cz in range(4):
            piece = window[16 * cz : 16 * cz + 16]
            shift = (32 * cz - first) % 128
            if shift:
                piece = pltpu.roll(piece, shift, 1)
            chunk = piece if chunk is None else jnp.where(group == cz, piece, chunk)
        out_ref[16 * d : 16 * d + 16, :] = chunk


def pack_kernel(r_ref, g_ref, before_ref, after_ref, up_ref, down_ref):
    received = r_ref[...]
    for ref in (up_ref, down_ref):
        ref[0:BASE, :] = received
        ref[PAYLOAD - 8 : PAYLOAD, :] = jnp.zeros((8, 128), F32)
    for p in range(4):
        ref = down_ref if p < 2 else up_ref
        for t in range(8):
            row = BASE + ((p % 2) * 8 + t) * EXT
            columns = slice(128 * t, 128 * t + 128)
            ref[row : row + 2, :] = before_ref[2 * p : 2 * p + 2, columns]
            ref[row + 2 : row + 34, :] = g_ref[p, :, columns]
            ref[row + 34 : row + 36, :] = after_ref[2 * p : 2 * p + 2, columns]
            ref[row + 36 : row + 40, :] = jnp.zeros((4, 128), F32)


def spectral_kernel(r_ref, fh_ref, fl_ref, out_ref):
    spaced = synth_x(fh_ref, fl_ref, r_ref[0:BASE, :])
    halves = []
    for half in (spaced[:, :128], spaced[:, 128:]):
        swapped = pltpu.roll(half, 64, 1)
        halves.append(
            jnp.where(
                lanes_of(half.shape) < 64, half * half - swapped * swapped, half * swapped
            )
        )
    products = jnp.concatenate(halves, axis=1)
    for first, row in ((0, 0), (128, HALF)):
        if row:
            products = products * sign_of(products.shape, 0)
        high, low = split(products)
        rows = slice(first, first + HALF)
        o = three(fh_ref[rows, :], fl_ref[rows, :], high, low)
        out_ref[row : row + HALF, :] = o[:, :128] + sign_of((HALF, 128), 0) * o[:, 128:]


def analysis_y_kernel(r_ref, fh_ref, fl_ref, out_ref):
    lane = lanes_of((16, 128))
    columns = []
    for t in range(6):
        rows = []
        for cz in range(4):
            tile = None
            for d in range(32):
                low, high = OWN * d - 128 * t, OWN * d - 128 * t + OWN
                if high <= 0 or low >= 128:
                    continue
                shift = (low - (32 * cz + 2)) % 128
                piece = r_ref[16 * d : 16 * d + 16, :]
                if shift:
                    piece = pltpu.roll(piece, shift, 1)
                tile = piece if tile is None else jnp.where(lane >= low, piece, tile)
            rows.append(tile)
        columns.append(jnp.concatenate(rows, axis=0))
    lines = jnp.concatenate(columns, axis=1)
    for first, column in ((0, 0), (128, HALF)):
        if column:
            lines = lines * sign_of(lines.shape, 1)
        high, low = split(lines)
        rows = [part[:, 384 * i : 384 * i + 384] for i in range(2) for part in (high, low)]
        o = mm(jnp.concatenate(rows, axis=0), fh_ref[:, first : first + HALF])
        p = mm(jnp.concatenate(rows[::2], axis=0), fl_ref[:, first : first + HALF])
        near = o[0:64] + o[64:128] + p[0:64]
        far = o[128:192] + o[192:256] + p[64:128]
        total = near + sign_of(far.shape, 1) * far
        out_ref[:, column : column + HALF] = (total * (1.0 / N)).astype(BF16)


def flux(g, gg, h):
    return (h - g) * (gg + h * h)


def fine_kernel(
    shift_ref,
    up_ref,
    down_ref,
    low_ref,
    high_ref,
    fh_ref,
    fl_ref,
    b_ref,
    out_ref,
    x_ref,
    u_ref,
    s_ref,
):
    below = low_ref[0:BASE, :]
    above = high_ref[0:BASE, :]
    left = lanes_of((BASE, 128)) < 64
    first = jnp.where(left, below, pltpu.roll(above, 64, 1))
    second = jnp.where(left, pltpu.roll(below, 64, 1), above)
    for i, lines in enumerate((first, second, up_ref[0:BASE, :])):
        points = synth_x(fh_ref, fl_ref, lines)
        x_ref[i, 0:384, :] = points[:, :128]
        x_ref[i, 384:N, :] = points[:, 128:]
        x_ref[i, N : N + 128, :] = points[0:128, :128]

    shift = shift_ref[0]
    base = lax.shift_right_arithmetic(3 * (1 + 2 * shift), 3) - 1
    cell = lax.broadcasted_iota(jnp.int32, (128, 128), 0)
    coarse = lanes_of((128, 128))
    numer = 3 * (2 * cell + 1 + 2 * shift)
    lower = lax.shift_right_arithmetic(numer, 3) - base
    t = jnp.bitwise_and(numer, 7).astype(F32) * 0.125
    square = t * t
    cube = square * t
    weights = (
        (-cube + 2.0 * square - t) * 0.5,
        (3.0 * cube - 5.0 * square + 2.0) * 0.5,
        (-3.0 * cube + 4.0 * square + t) * 0.5,
        (cube - square) * 0.5,
    )
    matrix = jnp.zeros((128, 128), F32)
    for offset, weight in zip(range(-1, 3), weights):
        matrix = matrix + jnp.where(coarse == lower + offset, weight, 0.0)
    wh, wl = split(matrix)
    both = jnp.concatenate([wh, wl], axis=0)

    for pair in range(4):
        lines = []
        for b in (2 * pair, 2 * pair + 1):
            start = lax.rem(base + N + 96 * b, N)
            window = jnp.concatenate([x_ref[i, pl.ds(start, 128), :] for i in range(3)], axis=1)
            vh, vl = split(window)
            o = mm(both, vh)
            lines.append(o[:128] + o[128:] + mm(wh, vl))
        lines = jnp.concatenate(lines, axis=0)
        for c in range(2):
            mine = jnp.concatenate([lines[:, 128 * c : 128 * c + 128], lines[:, 256:]], axis=1)
            vh, vl = split(mine)
            o = mm_nt(b_ref[c], vh)
            o = o[:240] + o[240:] + mm_nt(b_ref[c, 0:240, :], vl)
            u_ref[c, 2 * pair] = o[:, :128]
            u_ref[c, 2 * pair + 1] = o[:, 128:]

    homes = ((low_ref, 0), (low_ref, 1), (down_ref, 0), (down_ref, 1))
    homes = homes + ((up_ref, 0), (up_ref, 1), (high_ref, 0), (high_ref, 1))

    def around(centre, west, east):
        lane = lanes_of(centre.shape)
        to_east = pltpu.roll(jnp.where(lane == 0, east, centre), 127, 1)
        to_west = pltpu.roll(jnp.where(lane == 127, west, centre), 1, 1)
        return to_west, to_east

    def rate(load, planes, count, skip, use):
        def one(t, carry):
            west_t = lax.rem(t + 7, 8)
            east_t = lax.rem(t + 1, 8)
            first = planes[0]
            g = load(first, t, skip, count)
            gg = 2.0 + g * g
            below = load(first - 1, t, skip, count)
            lower = -flux(g, gg, below)
            for p in planes:
                above = load(p + 1, t, skip, count)
                north = load(p, t, skip + 1, count)
                south = load(p, t, skip - 1, count)
                west, east = around(
                    g, load(p, west_t, skip, count), load(p, east_t, skip, count)
                )
                row = (p - 1) * EXT + skip
                total = u_ref[0, t, row : row + count, :] * (east - west)
                total = total + u_ref[1, t, row : row + count, :] * (north - south)
                total = total + flux(g, gg, north) + flux(g, gg, south)
                total = total + flux(g, gg, east) + flux(g, gg, west)
                square = above * above
                upper = (above - g) * (gg + square)
                total = total + upper - lower
                use(p, t, g, g + 0.01 * total)
                lower, g, gg = upper, above, 2.0 + square
            return carry

        lax.fori_loop(0, 8, one, 0, unroll=2)

    def load_scalar(p, t, skip, count):
        ref, plane = homes[p]
        row = pl.multiple_of(BASE + (plane * 8 + t) * EXT, 8)
        return ref[pl.ds(row + skip, count), :]

    def load_section(p, t, skip, count):
        row = pl.multiple_of(((p - 1) * 8 + t) * EXT, 8)
        return s_ref[pl.ds(row + skip, count), :]

    def keep_section(p, t, g, result):
        row = pl.multiple_of(((p - 1) * 8 + t) * EXT, 8)
        s_ref[pl.ds(row, EXT), :] = result

    def keep_result(p, t, g, result):
        scalar = load_scalar(p, t, 2, 32)
        column = pl.multiple_of(t * 128, 128)
        out_ref[p - 2, :, pl.ds(column, 128)] = 0.5 * (scalar + result)

    rate(load_scalar, range(1, 7), EXT, 0, keep_section)
    rate(load_section, range(2, 6), 32, 2, keep_result)


def call(kernel, outs, flops, limit, scratch=(), smem=0, home=pltpu.VMEM):
    vmem = pl.BlockSpec(memory_space=pltpu.VMEM)
    place = pl.BlockSpec(memory_space=home)

    def run(*args):
        specs = [pl.BlockSpec(memory_space=pltpu.SMEM)] * smem + [place] * (len(args) - smem)
        size = sum(math.prod(a.shape) * a.dtype.itemsize for a in args)
        return pl.pallas_call(
            kernel,
            out_shape=outs,
            in_specs=specs,
            out_specs=jax.tree.map(lambda _: vmem, outs),
            scratch_shapes=scratch,
            compiler_params=pltpu.CompilerParams(vmem_limit_bytes=limit * 2**20),
            cost_estimate=pl.CostEstimate(flops=flops, bytes_accessed=size, transcendentals=0),
        )(*args)

    return run


def shards(velocity_modes, scalar, nest_shift):
    stencil = jnp.asarray(np.concatenate(split_host(-10.0 * row_plane_matrix()), axis=1))
    of = jax.ShapeDtypeStruct

    def ring(axis):
        count = lax.axis_size(axis)
        up = [(i, (i + 1) % count) for i in range(count)]
        return up, [(b, a) for a, b in up]

    def exchange(block):
        block = block.reshape(32, 16, 128)
        return lax.all_to_all(block, "wa", split_axis=0, concat_axis=0, tiled=True).reshape(512, 128)

    modes = velocity_modes.reshape(64, 512)
    seeds = jnp.asarray(cas_seeds())
    table = (pltpu.VMEM((N // 2, N // 2), BF16),) * 2
    sent = call(
        synth_y_kernel,
        of((512, 128), F32),
        10**9,
        60,
        scratch=table
        + (
            pltpu.VMEM((208, 128), F32),
            pltpu.VMEM((64, 512), F32),
            pltpu.SemaphoreType.DMA(()),
        ),
        home=pltpu.HBM,
    )(modes)
    received = exchange(sent)

    up, down = ring("wa")
    before = lax.ppermute(scalar[:, 30:32, :].reshape(8, 1024), "wa", up)
    after = lax.ppermute(scalar[:, 0:2, :].reshape(8, 1024), "wa", down)

    quarter = of((N // 2, N // 2), BF16)
    fh, fl = call(make_table, (quarter, quarter), 10**7, 8)(seeds)

    payload = of((PAYLOAD, 128), F32)
    to_up, to_down = call(pack_kernel, (payload, payload), 10**6, 8)(
        received, scalar, before, after
    )
    up, down = ring("gz")
    from_low = lax.ppermute(to_up, "gz", up)
    from_high = lax.ppermute(to_down, "gz", down)

    half = call(spectral_kernel, of((512, 128), F32), 10**9, 12)(
        to_up, fh, fl
    )
    returned = exchange(half)

    scalar_next = call(
        fine_kernel,
        of((4, 32, 1024), F32),
        2 * 10**9,
        24,
        scratch=(
            pltpu.VMEM((3, N + 128, 128), F32),
            pltpu.VMEM((2, 8, 6 * EXT, 128), F32),
            pltpu.VMEM((6 * 8 * EXT + 8, 128), F32),
        ),
        smem=1,
    )(nest_shift, to_up, to_down, from_low, from_high, fh, fl, stencil)

    stress = call(analysis_y_kernel, of((64, 512), BF16), 10**9, 8)(returned, fh, fl)
    return (stress.reshape(2, 2, 16, 512), scalar_next)


def solution(mesh):
    placed = (P(None, "gz", "wa", None), P("gz", "wa", None), P())
    return jax.shard_map(
        shards,
        mesh=mesh,
        in_specs=placed,
        out_specs=(P(None, "gz", "wa", None), P("gz", "wa", None)),
        check_vma=False,
    )
```
